32 devices in a mesh: groups: 2 (over x), row: 8 (over z, y), col: 2 (over core).
Axes of the slice: x: 2, y: 2, z: 4, core: 2. Of those that a mesh axis runs over, the one named last changes fastest.
Arguments:
- pair_rep: bfloat16 [160, 80, 128], P(('groups', 'row'), 'col'), parts along dimension 0, as said below
- proj_weight: bfloat16 [128, 512], replicated, may hold values from -0.5 to 0.5
- gate_weight: bfloat16 [128, 128], replicated, may hold values from -0.5 to 0.5
- out_weight: bfloat16 [128, 128], replicated, may hold values from -0.5 to 0.5
Outputs:
- update: bfloat16 [160, 80, 128], P(('groups', 'row'), 'col'), parts along dimension 0
The draws below stay inside these ranges and needn't reach their ends.
There are 2 independent parts, one for each index of `groups`. The reference program is written for one: setup_inputs(seed, part) draws one part's arguments, and reference() takes and returns one part's arrays. A program takes and returns all parts, laid end to end along the dimension named above; an argument that names none is the same for every part. Nothing has to cross between parts.
Inputs may be any that keep to these rules, and one draw needn't show every extreme that they name: `pair_rep`: real-valued pair features; each pair position and each channel carries its own scale factor between 1 and 10.
All inputs are finite; a program needn't handle non-finite values.
Results may differ from the reference program's by a relative error of at most 0.0078.
Values may be sent and summed in bfloat16 or wider, within the bound.
A program may use at most 128 MiB of HBM per device.

```python
import math
import jax
import jax.numpy as jnp
from jax import lax

C = 128
CH = 128
L = 80


def draw_pair_rep(key, part):
    first, second, third = jax.random.split(key, 3)
    position_scale = jnp.exp(jax.random.uniform(second, (L, L, 1), jnp.float32, 0.0, math.log(10.0)))
    channel_scale = jnp.exp(jax.random.uniform(third, (C,), jnp.float32, 0.0, math.log(10.0)))
    base = jax.random.normal(first, (L, L, C), jnp.float32)
    return (base * position_scale * channel_scale).astype(jnp.bfloat16)


def bell_draw(rng, dims, deviation, bound, kind=jnp.bfloat16):
    drawn = jax.random.normal(rng, dims, jnp.float32) * deviation
    return jnp.minimum(jnp.maximum(drawn, -bound), bound).astype(kind)


def setup_inputs(seed: int = 0, part: int = 0) -> dict:
    seeds = jax.random.split(jax.random.key(seed), 5)
    part_keys = jax.random.split(jax.random.fold_in(seeds[4], part), 5)
    pair_rep = draw_pair_rep(jax.random.fold_in(jax.random.fold_in(seeds[4], part), 71), part)
    proj_weight = bell_draw(seeds[1], (C, 4 * CH), C ** -0.5, 0.5)
    gate_weight = bell_draw(seeds[2], (C, C), C ** -0.5, 0.5)
    out_weight = bell_draw(seeds[3], (CH, C), CH ** -0.5, 0.5)
    return dict(pair_rep=pair_rep, proj_weight=proj_weight, gate_weight=gate_weight, out_weight=out_weight)


def layer_norm(values):
    average = lax.optimization_barrier(jnp.mean(values, axis=-1, keepdims=True))
    centered = values - average
    spread = lax.optimization_barrier(jnp.mean(centered * centered, axis=-1, keepdims=True))
    return centered * lax.rsqrt(spread + 1e-05)

def reference(pair_rep, proj_weight, gate_weight, out_weight):
    normed = layer_norm(pair_rep.astype(jnp.float32)).astype(jnp.bfloat16)
    flat_rows = normed.reshape(-1, C)
    projected = jnp.dot(flat_rows, proj_weight, preferred_element_type=jnp.float32)
    left_side = (jax.nn.sigmoid(projected[:, :CH]) * projected[:, CH:2 * CH]).astype(jnp.bfloat16)
    right_side = (jax.nn.sigmoid(projected[:, 2 * CH:3 * CH]) * projected[:, 3 * CH:]).astype(jnp.bfloat16)
    left_side = left_side.reshape(L, L, CH).astype(jnp.float32)
    right_side = right_side.reshape(L, L, CH).astype(jnp.float32)
    combined = jnp.einsum('ikc,jkc->ijc', left_side, right_side)
    tri_normed = layer_norm(combined).astype(jnp.bfloat16).reshape(-1, CH)
    gating = jax.nn.sigmoid(jnp.dot(flat_rows, gate_weight, preferred_element_type=jnp.float32))
    update = jnp.dot(tri_normed, out_weight, preferred_element_type=jnp.float32) * gating
    return update.astype(jnp.bfloat16).reshape(L, L, C)
```

```python
import functools

import jax
import jax.numpy as jnp
from jax import lax
from jax.experimental import pallas as pl
from jax.experimental.pallas import tpu as pltpu
from jax.sharding import PartitionSpec as P

MESH = pl.DeviceIdType.MESH
F32 = jnp.float32
BF16 = jnp.bfloat16


def layer_norm(values):
    average = jnp.mean(values, axis=-1, keepdims=True)
    centered = values - average
    spread = jnp.mean(centered * centered, axis=-1, keepdims=True)
    return centered * lax.rsqrt(spread + 1e-05)


def kernel(
    n, rows, cols, pairs, x_hbm, wp_hbm, wg_hbm, wo_hbm, out_ref,
    x_ref, wp_ref, wg_ref, wo_ref, normed, in_sem, own, right, left, left32, comb, gate, stage, back,
    own_send, fwd_send, recv, lsend, lrecv, ret_send, ret_recv,
):
    hid = wo_ref.shape[0]
    flat = rows * cols
    step = flat // pairs
    loads = [pltpu.make_async_copy(x_hbm, x_ref, in_sem.at[0])]
    for k in (1, 0):
        cut = (slice(None), pl.ds(2 * hid * k, 2 * hid))
        loads.append(pltpu.make_async_copy(wp_hbm.at[cut], wp_ref.at[k], in_sem.at[len(loads)]))
    loads.append(pltpu.make_async_copy(wg_hbm, wg_ref, in_sem.at[3]))
    loads.append(pltpu.make_async_copy(wo_hbm, wo_ref, in_sem.at[4]))
    for load in loads:
        load.start()
    deep = n // 2
    span = deep // 2
    row, c = lax.axis_index("row"), lax.axis_index("col")
    z, y = row // 2, row % 2
    across = 2 * z + 1 - y
    has_up, has_down, has_far = z < deep - 1, z > 0, z > 2
    low = c * span
    dest = z // span
    my_slot = z - dest * span
    barrier = pltpu.get_barrier_semaphore()

    def greet(r, cc):
        pl.semaphore_signal(barrier, inc=1, device_id={"row": r, "col": cc}, device_id_type=MESH)

    @pl.when((z + 3 < deep) & ((z + 3) // span == c))
    def _():
        for cc in range(2):
            greet(row + 6, cc)

    @pl.when(has_up)
    def _():
        for cc in range(2):
            greet(row + 2, cc)

    @pl.when(has_down)
    def _():
        for cc in range(2):
            greet(row - 2, cc)

    greet(across, c)
    greet(row, 1 - c)

    def gated(values, k):
        proj = jnp.dot(values, wp_ref[k], preferred_element_type=F32)
        return (jax.nn.sigmoid(proj[:, :hid]) * proj[:, hid:]).astype(BF16)

    def prepare(p):
        here = pl.ds(p * step, step)
        values = layer_norm(x_ref[here, :].astype(F32)).astype(BF16)
        normed[here, :] = values
        own[here, :] = gated(values, 1)

    loads[0].wait()
    loads[1].wait()

    ways = ((0, has_far, row - 6, dest), (1, has_up, row + 2, dest), (2, has_down, row - 2, dest), (3, dest != c, row, dest))

    def own_copy(way, r, cc, part):
        return pltpu.make_async_remote_copy(
            src_ref=own.at[part], dst_ref=right.at[my_slot, c, part],
            send_sem=own_send.at[way], recv_sem=recv.at[my_slot, part.start // step],
            device_id={"row": r, "col": cc}, device_id_type=MESH,
        )

    for p in range(pairs):
        prepare(p)
    def compute_left():
        loads[2].wait()
        left[y, c] = gated(normed[...], 0)

    @pl.when(has_up)
    def _():
        compute_left()
    pl.semaphore_wait(barrier, 2 + 2 * has_up.astype(jnp.int32) + 2 * has_down.astype(jnp.int32) + has_far.astype(jnp.int32))
    for p in range(pairs):
        for way, cond, r, cc in ways:
            @pl.when(cond)
            def _(way=way, r=r, cc=cc):
                own_copy(way, r, cc, pl.ds(p * step, step)).start()

    @pl.when(dest == c)
    def _():
        right[my_slot, c] = own[...]

    def left_copy(which, kc, way, arrive, r, cc):
        part = left.at[which, kc]
        return pltpu.make_async_remote_copy(
            src_ref=part, dst_ref=part, send_sem=lsend.at[way], recv_sem=lrecv.at[arrive],
            device_id={"row": r, "col": cc}, device_id_type=MESH,
        )

    to_across = left_copy(y, c, 0, 0, across, c)
    to_sibling = left_copy(y, c, 1, 1, row, 1 - c)
    passed_on = left_copy(1 - y, c, 2, 1, row, 1 - c)
    @pl.when(jnp.logical_not(has_up))
    def _():
        compute_left()
    to_across.start()
    to_sibling.start()
    left32[y, c] = left[y, c].astype(F32)
    loads[3].wait()
    gate[...] = jax.nn.sigmoid(jnp.dot(normed[...], wg_ref[...], preferred_element_type=F32))

    def source(t):
        inside = low + lax.rem(z - low + t + 1 + deep, span)
        return jnp.where(z < low, low + t, jnp.where(z >= low + span, low + span - 1 - t, inside))

    def passes(zs):
        return ((zs < z) & has_up) | (((zs == z + 1) | (zs > z + 2)) & has_down)

    def block(part, slot, q, r):
        return pltpu.make_async_remote_copy(
            src_ref=part, dst_ref=part, send_sem=fwd_send.at[slot],
            recv_sem=recv.at[slot, q], device_id={"row": r, "col": c}, device_id_type=MESH,
        )

    def both(slot, q):
        return right.at[slot, :, pl.ds(q * step, step)]

    def send_on(t, start, stop):
        zs = source(t)
        slot = zs - low

        @pl.when(passes(zs))
        def _():
            @pl.loop(start, stop)
            def _(q):
                block(both(slot, q), slot, q, row).wait_recv()
                block(both(slot, q), slot, q, jnp.where(zs < z, row + 2, row - 2)).start()

    early = jnp.where(c == 0, pairs, pairs - 2)
    send_on(0, 0, early)
    left_copy(1 - y, c, 0, 0, across, c).wait_recv()
    passed_on.start()
    send_on(0, early, pairs)
    pl.loop(1, span)(lambda t: send_on(t, 0, pairs))
    left32[1 - y, c] = left[1 - y, c].astype(F32)
    pltpu.make_async_remote_copy(
        src_ref=left.at[:, 1 - c], dst_ref=left.at[:, 1 - c], send_sem=lsend.at[1], recv_sem=lrecv.at[1],
        device_id={"row": row, "col": 1 - c}, device_id_type=MESH,
    ).wait_recv()
    for which in range(2):
        left32[which, 1 - c] = left[which, 1 - c].astype(F32)

    def ret_copy(part, there, slot):
        return pltpu.make_async_remote_copy(
            src_ref=part, dst_ref=there, send_sem=ret_send, recv_sem=ret_recv.at[slot],
            device_id={"row": across, "col": c}, device_id_type=MESH,
        )

    def sums(which, slot, pair, put):
        acc = [[None, None] for _ in range(rows)]
        for kc in range(2):
            wide = right[slot, kc, pl.ds(pair * 2 * cols, 2 * cols), :].astype(F32)
            for kt in range(0, cols, 8):
                r = [wide[j * cols + kt : j * cols + kt + 8] for j in range(2)]
                for i in range(rows):
                    l = left32[which, kc, i * cols + kt : i * cols + kt + 8, :]
                    for j in range(2):
                        term = l * r[j]
                        acc[i][j] = term if acc[i][j] is None else acc[i][j] + term
        for i in range(rows):
            for j in range(2):
                put(i, j, jnp.sum(acc[i][j], axis=0, keepdims=True))

    def place(i, j, slot, pair, side, value):
        comb[pl.ds(i * cols + (slot * 2 + side) * rows + pair * 2 + j, 1), :] = value

    def order(t):
        return source(lax.rem(t + jnp.where((z >= low) & (z < low + span), span - 1, 0), span))

    @pl.loop(0, pairs)
    def _(pair):
        @pl.loop(0, span)
        def _(t):
            zs = order(t)
            slot = zs - low
            @pl.when((zs == z) & jnp.logical_not(passes(zs)))
            def _():
                block(right.at[slot, 1 - c, pl.ds(pair * step, step)], slot, pair, row).wait_recv()

            @pl.when((zs != z) & jnp.logical_not(passes(zs)))
            def _():
                block(both(slot, pair), slot, pair, row).wait_recv()

            def put_stage(i, j, value):
                stage[slot, pair, j * rows + i : j * rows + i + 1, :] = value

            sums(1 - y, slot, pair, put_stage)
            ret_copy(stage.at[slot, pair], back.at[slot, pair], slot).start()
            sums(y, slot, pair, lambda i, j, value: place(i, j, slot, pair, y, value))

    for way, cond, r, cc in ways:
        @pl.when(cond)
        def _(way=way, r=r, cc=cc):
            own_copy(way, r, cc, pl.ds(0, flat)).wait_send()
    for copy in (to_across, to_sibling, passed_on):
        copy.wait_send()

    @pl.loop(0, span)
    def _(slot):
        @pl.when(passes(slot + low))
        def _():
            block(right.at[slot], slot, 0, row).wait_send()

    @pl.loop(0, span)
    def _(t):
        slot = order(t) - low
        ret_copy(stage.at[slot], back.at[slot], slot).wait_recv()

        @pl.loop(0, pairs)
        def _(pair):
            for i in range(rows):
                for j in range(2):
                    got = back[slot, pair, j * rows + i : j * rows + i + 1, :]
                    place(i, j, slot, pair, 1 - y, got)

    ret_copy(stage, back, 0).wait_send()
    loads[4].wait()
    tri = layer_norm(comb[...]).astype(BF16)
    update = jnp.dot(tri, wo_ref[...], preferred_element_type=F32) * gate[...]
    out_ref[...] = update.astype(BF16)


def per_device(n, pair_rep, proj_weight, gate_weight, out_weight):
    rows, cols, channels = pair_rep.shape
    hid = out_weight.shape[0]
    flat = rows * cols
    pairs = rows // 2
    span = n // 4
    padded = -(-2 * rows // 8) * 8
    vmem = pl.BlockSpec(memory_space=pltpu.VMEM)
    dma = pltpu.SemaphoreType.DMA
    out = pl.pallas_call(
        functools.partial(kernel, n, rows, cols, pairs),
        out_shape=pltpu.VMEM((flat, channels), BF16),
        in_specs=[pl.BlockSpec(memory_space=pl.ANY)] * 4,
        out_specs=vmem,
        scratch_shapes=[
            pltpu.VMEM((flat, channels), BF16),
            pltpu.VMEM((2, channels, 2 * hid), BF16),
            pltpu.VMEM((channels, channels), BF16),
            pltpu.VMEM((hid, channels), BF16),
            pltpu.VMEM((flat, channels), BF16),
            dma((5,)),
            pltpu.VMEM((flat, hid), BF16),
            pltpu.VMEM((span, 2, flat, hid), BF16),
            pltpu.VMEM((2, 2, flat, hid), BF16),
            pltpu.VMEM((2, 2, flat, hid), F32),
            pltpu.VMEM((flat, hid), F32),
            pltpu.VMEM((flat, channels), F32),
            pltpu.VMEM((span, pairs, padded, hid), F32),
            pltpu.VMEM((span, pairs, padded, hid), F32),
            dma((4,)),
            dma((span,)),
            dma((span, pairs)),
            dma((3,)),
            dma((2,)),
            dma,
            dma((span,)),
        ],
        compiler_params=pltpu.CompilerParams(
            collective_id=0, has_side_effects=True, vmem_limit_bytes=60 * 1024 * 1024
        ),
    )(pair_rep.reshape(flat, channels), proj_weight, gate_weight, out_weight)
    return out.reshape(rows, cols, channels)


def solution(mesh):
    placed = (P(("groups", "row"), "col", None), P(), P(), P())
    return jax.shard_map(
        functools.partial(per_device, mesh.shape["row"]),
        mesh=mesh,
        in_specs=placed,
        out_specs=P(("groups", "row"), "col", None),
        check_vma=False,
    )
```

```python
import functools

import jax
import jax.numpy as jnp
from jax import lax
from jax.experimental import pallas as pl
from jax.experimental.pallas import tpu as pltpu
from jax.sharding import PartitionSpec as P

MESH = pl.DeviceIdType.MESH
F32 = jnp.float32
BF16 = jnp.bfloat16


def layer_norm(values):
    average = jnp.mean(values, axis=-1, keepdims=True)
    centered = values - average
    spread = jnp.mean(centered * centered, axis=-1, keepdims=True)
    return centered * lax.rsqrt(spread + 1e-05)


def kernel(
    n, rows, cols, pairs, twice, x_hbm, wp_hbm, wg_hbm, wo_hbm, out_ref,
    x_ref, wp_ref, wg_ref, wo_ref, normed, in_sem, own, right, left, left32, comb, gate, stage, back, other,
    own_send, fwd_send, recv, lsend, lrecv, ret_send, ret_recv, other_send, other_recv,
):
    hid = wo_ref.shape[0]
    flat = rows * cols
    step = flat // pairs
    loads = [pltpu.make_async_copy(x_hbm, x_ref, in_sem.at[0])]
    for k in (1, 0):
        cut = (slice(None), pl.ds(2 * hid * k, 2 * hid))
        loads.append(pltpu.make_async_copy(wp_hbm.at[cut], wp_ref.at[k], in_sem.at[len(loads)]))
    loads.append(pltpu.make_async_copy(wg_hbm, wg_ref, in_sem.at[3]))
    loads.append(pltpu.make_async_copy(wo_hbm, wo_ref, in_sem.at[4]))
    for load in loads:
        load.start()
    deep = n // 2
    span = deep // 2
    row, c = lax.axis_index("row"), lax.axis_index("col")
    z, y = row // 2, row % 2
    across = 2 * z + 1 - y
    has_up, has_down, has_far = z < deep - 1, z > 0, z > 2
    low = c * span
    dest = z // span
    my_slot = z - dest * span
    once = pairs - twice
    far = (z < low) | (z >= low + span)
    helped = far & (y == 0)
    target = z + 1 - 2 * c
    helps = (y == 1) & jnp.where(c == 1, (z >= 1) & (z <= span), (z >= span - 1) & (z < deep - 1))
    barrier = pltpu.get_barrier_semaphore()

    def greet(r, cc):
        pl.semaphore_signal(barrier, inc=1, device_id={"row": r, "col": cc}, device_id_type=MESH)

    @pl.when((z + 3 < deep) & ((z + 3) // span == c))
    def _():
        for cc in range(2):
            greet(row + 6, cc)

    @pl.when(has_up)
    def _():
        for cc in range(2):
            greet(row + 2, cc)

    @pl.when(has_down)
    def _():
        for cc in range(2):
            greet(row - 2, cc)

    @pl.when(helped)
    def _():
        greet(2 * (z - 1 + 2 * c) + 1, c)

    greet(across, c)
    greet(row, 1 - c)

    def gated(values, k):
        proj = jnp.dot(values, wp_ref[k], preferred_element_type=F32)
        return (jax.nn.sigmoid(proj[:, :hid]) * proj[:, hid:]).astype(BF16)

    def prepare(p):
        here = pl.ds(p * step, step)
        values = layer_norm(x_ref[here, :].astype(F32)).astype(BF16)
        normed[here, :] = values
        own[here, :] = gated(values, 1)

    loads[0].wait()
    loads[1].wait()

    ways = ((0, has_far, row - 6, dest), (1, has_up, row + 2, dest), (2, has_down, row - 2, dest), (3, dest != c, row, dest))

    def own_copy(way, r, cc, part):
        return pltpu.make_async_remote_copy(
            src_ref=own.at[part], dst_ref=right.at[my_slot, c, part],
            send_sem=own_send.at[way], recv_sem=recv.at[my_slot, part.start // step],
            device_id={"row": r, "col": cc}, device_id_type=MESH,
        )

    for p in range(pairs):
        prepare(p)
    def compute_left():
        loads[2].wait()
        left[y, c] = gated(normed[...], 0)

    @pl.when(has_up)
    def _():
        compute_left()
    pl.semaphore_wait(barrier, 2 + 2 * has_up.astype(jnp.int32) + 2 * has_down.astype(jnp.int32) + has_far.astype(jnp.int32) + helps.astype(jnp.int32))
    for p in range(pairs):
        for way, cond, r, cc in ways:
            @pl.when(cond)
            def _(way=way, r=r, cc=cc):
                own_copy(way, r, cc, pl.ds(p * step, step)).start()

    @pl.when(dest == c)
    def _():
        right[my_slot, c] = own[...]

    def left_copy(which, kc, way, arrive, r, cc):
        part = left.at[which, kc]
        return pltpu.make_async_remote_copy(
            src_ref=part, dst_ref=part, send_sem=lsend.at[way], recv_sem=lrecv.at[arrive],
            device_id={"row": r, "col": cc}, device_id_type=MESH,
        )

    to_across = left_copy(y, c, 0, 0, across, c)
    to_sibling = left_copy(y, c, 1, 1, row, 1 - c)
    passed_on = left_copy(1 - y, c, 2, 1, row, 1 - c)
    @pl.when(jnp.logical_not(has_up))
    def _():
        compute_left()
    to_across.start()
    to_sibling.start()
    left32[y, c] = left[y, c].astype(F32)
    loads[3].wait()
    opened = jax.nn.sigmoid(jnp.dot(normed[...], wg_ref[...], preferred_element_type=F32))
    gate[...] = opened.reshape(rows, cols, -1)

    def source(t):
        inside = low + lax.rem(z - low + t + 1 + deep, span)
        return jnp.where(z < low, low + t, jnp.where(z >= low + span, low + span - 1 - t, inside))

    def passes(zs):
        return ((zs < z) & has_up) | (((zs == z + 1) | (zs > z + 2)) & has_down)

    def block(part, slot, q, r):
        return pltpu.make_async_remote_copy(
            src_ref=part, dst_ref=part, send_sem=fwd_send.at[slot],
            recv_sem=recv.at[slot, q], device_id={"row": r, "col": c}, device_id_type=MESH,
        )

    def both(slot, q):
        return right.at[slot, :, pl.ds(q * step, step)]

    def other_copy(slot, d, count):
        return pltpu.make_async_remote_copy(
            src_ref=right.at[slot, :, pl.ds((once + d) * step, count * step)],
            dst_ref=other.at[:, pl.ds(d * step, count * step)],
            send_sem=other_send, recv_sem=other_recv.at[d], device_id={"row": 2 * target, "col": c}, device_id_type=MESH,
        )

    shared = jnp.where(c == 1, jnp.where(target == 0, span, deep - 1), 0)

    def send_on(t, start, stop):
        zs = source(t)
        slot = zs - low

        @pl.when(passes(zs))
        def _():
            @pl.loop(start, stop)
            def _(q):
                block(both(slot, q), slot, q, row).wait_recv()
                @pl.when(helps & (zs == shared) & (q >= once))
                def _():
                    other_copy(slot, q - once, 1).start()

                block(both(slot, q), slot, q, jnp.where(zs < z, row + 2, row - 2)).start()

    early = jnp.where(c == 0, pairs, 0)
    send_on(0, 0, early)
    left_copy(1 - y, c, 0, 0, across, c).wait_recv()
    passed_on.start()
    send_on(0, early, pairs)
    pl.loop(1, span)(lambda t: send_on(t, 0, pairs))
    left32[1 - y, c] = left[1 - y, c].astype(F32)
    pltpu.make_async_remote_copy(
        src_ref=left.at[:, 1 - c], dst_ref=left.at[:, 1 - c], send_sem=lsend.at[1], recv_sem=lrecv.at[1],
        device_id={"row": row, "col": 1 - c}, device_id_type=MESH,
    ).wait_recv()
    for which in range(2):
        left32[which, 1 - c] = left[which, 1 - c].astype(F32)

    def ret_copy(part, there, slot):
        return pltpu.make_async_remote_copy(
            src_ref=part, dst_ref=there, send_sem=ret_send.at[slot], recv_sem=ret_recv.at[slot],
            device_id={"row": across, "col": c}, device_id_type=MESH,
        )

    def sums(which, blocks, pair, put):
        acc = [[None, None] for _ in range(rows)]
        for kc in range(2):
            wide = blocks[kc, pl.ds(pair * 2 * cols, 2 * cols), :].astype(F32)
            for kt in range(0, cols, 8):
                r = [wide[j * cols + kt : j * cols + kt + 8] for j in range(2)]
                for i in range(rows):
                    l = left32[which, kc, i * cols + kt : i * cols + kt + 8, :]
                    for j in range(2):
                        term = l * r[j]
                        acc[i][j] = term if acc[i][j] is None else acc[i][j] + term
        for i in range(rows):
            for j in range(2):
                put(i, j, jnp.sum(acc[i][j], axis=0, keepdims=True))

    def place(i, j, slot, pair, side, value):
        comb[i, pl.ds((slot * 2 + side) * rows + pair * 2 + j, 1), :] = value

    def order(t):
        inside = lax.rem(t + span - 1, span)
        return source(jnp.where((z >= low) & (z < low + span), inside, jnp.where(z > 0, t, span - 1 - t)))

    last = order(span - 1) - low

    @pl.loop(0, span)
    def _(t):
        zs = order(t)
        slot = zs - low
        kept = jnp.where(far & (y == 1) & (slot == last), once, pairs)

        @pl.loop(0, pairs)
        def _(pair):
            @pl.when((zs == z) & jnp.logical_not(passes(zs)))
            def _():
                block(right.at[slot, 1 - c, pl.ds(pair * step, step)], slot, pair, row).wait_recv()

            @pl.when((zs != z) & jnp.logical_not(passes(zs)))
            def _():
                block(both(slot, pair), slot, pair, row).wait_recv()

            def put_stage(i, j, value):
                stage[slot, pair, j * rows + i : j * rows + i + 1, :] = value

            @pl.when(pair < kept)
            def _():
                sums(1 - y, right.at[slot], pair, put_stage)
                ret_copy(stage.at[slot, pair], back.at[slot, pair], slot).start()

            sums(y, right.at[slot], pair, lambda i, j, value: place(i, j, slot, pair, y, value))


    for way, cond, r, cc in ways:
        @pl.when(cond)
        def _(way=way, r=r, cc=cc):
            own_copy(way, r, cc, pl.ds(0, flat)).wait_send()
    for copy in (to_across, to_sibling, passed_on):
        copy.wait_send()

    @pl.loop(0, span)
    def _(slot):
        @pl.when(passes(slot + low))
        def _():
            block(right.at[slot], slot, 0, row).wait_send()

    @pl.when(helps)
    def _():
        other_copy(shared - low, 0, twice).wait_send()

    def collect(slot, part, stop):
        ret_copy(stage.at[slot, part], back.at[slot, part], slot).wait_recv()

        @pl.loop(0, stop)
        def _(pair):
            for i in range(rows):
                for j in range(2):
                    got = back[slot, pair, j * rows + i : j * rows + i + 1, :]
                    place(i, j, slot, pair, 1 - y, got)

    def finish(start, width):
        here = (slice(None), pl.ds(pl.multiple_of(start, 8), width))
        tri = layer_norm(comb[here].reshape(rows * width, hid)).astype(BF16)
        update = jnp.dot(tri, wo_ref[...], preferred_element_type=F32) * gate[here].reshape(rows * width, -1)
        out_ref[here] = update.astype(BF16).reshape(rows, width, -1)

    wide = 2 * rows
    width = max(-(-(s * wide % 8 + wide) // 8) * 8 for s in range(span))
    start = jnp.minimum(last * wide // 8 * 8, cols - width)
    every = pl.ds(0, pairs)
    some = pl.ds(0, once)

    @pl.loop(0, twice)
    def _(d):
        @pl.when(d == twice - 1)
        def _():
            pl.loop(0, span - 1)(lambda t: collect(order(t) - low, every, pairs))
            loads[4].wait()
            if span == 2:
                finish(jnp.where(start == 0, width, 0), cols - width)
            else:
                @pl.loop(0, cols // 8)
                def _(b):
                    @pl.when((8 * b < start) | (8 * b >= start + width))
                    def _():
                        finish(8 * b, 8)

        @pl.when(helped)
        def _():
            other_copy(last, d, 1).wait_recv()
            sums(y, other, d, lambda i, j, value: place(i, j, last, once + d, 1 - y, value))

    pl.when(helped)(lambda: collect(last, some, once))
    pl.when(jnp.logical_not(helped))(lambda: collect(last, every, pairs))
    finish(start, width)
    @pl.loop(0, span)
    def _(slot):
        kept = far & (y == 1) & (slot == last)
        pl.when(kept)(lambda: ret_copy(stage.at[slot, some], back.at[slot, some], slot).wait_send())
        pl.when(jnp.logical_not(kept))(lambda: ret_copy(stage.at[slot], back.at[slot], slot).wait_send())


def per_device(n, pair_rep, proj_weight, gate_weight, out_weight):
    rows, cols, channels = pair_rep.shape
    hid = out_weight.shape[0]
    flat = rows * cols
    pairs = rows // 2
    twice = pairs // 2
    span = n // 4
    padded = -(-2 * rows // 8) * 8
    vmem = pl.BlockSpec(memory_space=pltpu.VMEM)
    dma = pltpu.SemaphoreType.DMA
    return pl.pallas_call(
        functools.partial(kernel, n, rows, cols, pairs, twice),
        out_shape=pltpu.VMEM((rows, cols, channels), BF16),
        in_specs=[pl.BlockSpec(memory_space=pl.ANY)] * 4,
        out_specs=vmem,
        scratch_shapes=[
            pltpu.VMEM((flat, channels), BF16),
            pltpu.VMEM((2, channels, 2 * hid), BF16),
            pltpu.VMEM((channels, channels), BF16),
            pltpu.VMEM((hid, channels), BF16),
            pltpu.VMEM((flat, channels), BF16),
            dma((5,)),
            pltpu.VMEM((flat, hid), BF16),
            pltpu.VMEM((span, 2, flat, hid), BF16),
            pltpu.VMEM((2, 2, flat, hid), BF16),
            pltpu.VMEM((2, 2, flat, hid), F32),
            pltpu.VMEM((rows, cols, hid), F32),
            pltpu.VMEM((rows, cols, channels), F32),
            pltpu.VMEM((span, pairs, padded, hid), F32),
            pltpu.VMEM((span, pairs, padded, hid), F32),
            pltpu.VMEM((2, twice * (flat // pairs), hid), BF16),
            dma((4,)),
            dma((span,)),
            dma((span, pairs)),
            dma((3,)),
            dma((2,)),
            dma((span,)),
            dma((span,)),
            dma,
            dma((twice,)),
        ],
        compiler_params=pltpu.CompilerParams(
            collective_id=0, has_side_effects=True, vmem_limit_bytes=60 * 1024 * 1024
        ),
    )(pair_rep.reshape(flat, channels), proj_weight, gate_weight, out_weight)


def solution(mesh):
    placed = (P(("groups", "row"), "col", None), P(), P(), P())
    return jax.shard_map(
        functools.partial(per_device, mesh.shape["row"]),
        mesh=mesh,
        in_specs=placed,
        out_specs=P(("groups", "row"), "col", None),
        check_vma=False,
    )
```

```python
import functools

import jax
import jax.numpy as jnp
from jax import lax
from jax.experimental import pallas as pl
from jax.experimental.pallas import tpu as pltpu
from jax.sharding import PartitionSpec as P

MESH = pl.DeviceIdType.MESH
F32 = jnp.float32
BF16 = jnp.bfloat16
TWICE = 3
LESS = 2


def layer_norm(values):
    average = jnp.mean(values, axis=-1, keepdims=True)
    centered = values - average
    spread = jnp.mean(centered * centered, axis=-1, keepdims=True)
    return centered * lax.rsqrt(spread + 1e-05)


def kernel(
    n, rows, cols, pairs, twice, x_hbm, wp_hbm, wg_hbm, wo_hbm, out_ref,
    x_ref, wp_ref, wg_ref, wo_ref, normed, in_sem, own, right, left, left32, comb, gate, stage, back, other,
    own_send, fwd_send, recv, lsend, lrecv, ret_send, ret_recv, other_send, other_recv,
):
    hid = wo_ref.shape[0]
    flat = rows * cols
    step = flat // pairs
    loads = [pltpu.make_async_copy(x_hbm, x_ref, in_sem.at[0])]
    for k in (1, 0):
        cut = (slice(None), pl.ds(2 * hid * k, 2 * hid))
        loads.append(pltpu.make_async_copy(wp_hbm.at[cut], wp_ref.at[k], in_sem.at[len(loads)]))
    loads.append(pltpu.make_async_copy(wg_hbm, wg_ref, in_sem.at[3]))
    loads.append(pltpu.make_async_copy(wo_hbm, wo_ref, in_sem.at[4]))
    for load in loads:
        load.start()
    deep = n // 2
    span = deep // 2
    row, c = lax.axis_index("row"), lax.axis_index("col")
    z, y = row // 2, row % 2
    across = 2 * z + 1 - y
    has_up, has_down, has_far = z < deep - 1, z > 0, z > 2
    low = c * span
    dest = z // span
    my_slot = z - dest * span
    far = (z < low) | (z >= low + span)

    def first_twice(chip):
        return pairs - jnp.where((chip == 0) & (c == 1), twice, LESS)

    once = first_twice(z)
    helped = far & (y == 0)
    target = z + 1 - 2 * c
    helps = (y == 1) & jnp.where(c == 1, (z >= 1) & (z <= span), (z >= span - 1) & (z < deep - 1))
    barrier = pltpu.get_barrier_semaphore()

    def greet(r, cc):
        pl.semaphore_signal(barrier, inc=1, device_id={"row": r, "col": cc}, device_id_type=MESH)

    @pl.when((z + 3 < deep) & ((z + 3) // span == c))
    def _():
        for cc in range(2):
            greet(row + 6, cc)

    @pl.when(has_up)
    def _():
        for cc in range(2):
            greet(row + 2, cc)

    @pl.when(has_down)
    def _():
        for cc in range(2):
            greet(row - 2, cc)

    @pl.when(helped)
    def _():
        greet(2 * (z - 1 + 2 * c) + 1, c)

    greet(across, c)
    greet(row, 1 - c)

    def gated(values, k):
        proj = jnp.dot(values, wp_ref[k], preferred_element_type=F32)
        return (jax.nn.sigmoid(proj[:, :hid]) * proj[:, hid:]).astype(BF16)

    def prepare(p):
        here = pl.ds(p * step, step)
        values = layer_norm(x_ref[here, :].astype(F32)).astype(BF16)
        normed[here, :] = values
        own[here, :] = gated(values, 1)

    loads[0].wait()
    loads[1].wait()

    ways = ((0, has_far, row - 6, dest), (1, has_up, row + 2, dest), (2, has_down, row - 2, dest), (3, dest != c, row, dest))

    def own_copy(way, r, cc, part):
        return pltpu.make_async_remote_copy(
            src_ref=own.at[part], dst_ref=right.at[my_slot, c, part],
            send_sem=own_send.at[way], recv_sem=recv.at[my_slot, part.start // step],
            device_id={"row": r, "col": cc}, device_id_type=MESH,
        )

    for p in range(pairs):
        prepare(p)
    def compute_left():
        loads[2].wait()
        left[2 * c + y] = gated(normed[...], 0)

    @pl.when(has_up)
    def _():
        compute_left()
    pl.semaphore_wait(barrier, 2 + 2 * has_up.astype(jnp.int32) + 2 * has_down.astype(jnp.int32) + has_far.astype(jnp.int32) + helps.astype(jnp.int32))
    for p in range(pairs):
        for way, cond, r, cc in ways:
            @pl.when(cond)
            def _(way=way, r=r, cc=cc):
                own_copy(way, r, cc, pl.ds(p * step, step)).start()

    @pl.when(dest == c)
    def _():
        right[my_slot, c] = own[...]

    def left_copy(which, kc, arrive, r, cc):
        part = left.at[2 * kc + which]
        return pltpu.make_async_remote_copy(
            src_ref=part, dst_ref=part, send_sem=lsend, recv_sem=lrecv.at[arrive],
            device_id={"row": r, "col": cc}, device_id_type=MESH,
        )

    to_across = left_copy(y, c, 0, across, c)
    to_sibling = left_copy(y, c, 1, row, 1 - c)
    passed_on = left_copy(1 - y, c, 1, row, 1 - c)
    @pl.when(jnp.logical_not(has_up))
    def _():
        compute_left()
    to_across.start()
    to_sibling.start()
    left32[y, c] = left[2 * c + y].astype(F32)
    loads[3].wait()
    opened = jax.nn.sigmoid(jnp.dot(normed[...], wg_ref[...], preferred_element_type=F32))
    gate[...] = opened.reshape(rows, cols, -1)

    def source(t):
        inside = low + lax.rem(z - low + t + 1 + deep, span)
        return jnp.where(z < low, low + t, jnp.where(z >= low + span, low + span - 1 - t, inside))

    def passes(zs):
        return ((zs < z) & has_up) | (((zs == z + 1) | (zs > z + 2)) & has_down)

    def block(part, slot, q, r):
        return pltpu.make_async_remote_copy(
            src_ref=part, dst_ref=part, send_sem=fwd_send.at[slot],
            recv_sem=recv.at[slot, q], device_id={"row": r, "col": c}, device_id_type=MESH,
        )

    def both(slot, q):
        return right.at[slot, :, pl.ds(q * step, step)]

    def other_copy(slot, d, count):
        return pltpu.make_async_remote_copy(
            src_ref=right.at[slot, :, pl.ds((once_there + d) * step, count * step)],
            dst_ref=other.at[:, pl.ds(d * step, count * step)],
            send_sem=other_send, recv_sem=other_recv.at[d], device_id={"row": 2 * target, "col": c}, device_id_type=MESH,
        )

    once_there = first_twice(target)
    shared = jnp.where(c == 1, jnp.where(target == 0, span, deep - 1), 0)

    def relay(zs, q):
        slot = zs - low
        to = jnp.where(zs < z, row + 2, row - 2)

        @pl.when(passes(zs))
        def _():
            doubled = helps & (zs == shared) & (q >= once_there)
            block(both(slot, q), slot, q, row).wait_recv()

            @pl.when(doubled)
            def _():
                other_copy(slot, q - once_there, 1).start()

            @pl.when(jnp.logical_not(doubled))
            def _():
                block(both(slot, q), slot, q, to).start()

            @pl.when(doubled & (q == pairs - 1))
            def _():
                pl.loop(once_there, pairs)(lambda p: block(both(slot, p), slot, p, to).start())

    early = jnp.where(c == 0, pairs, 0)
    pl.loop(0, early)(lambda q: relay(source(0), q))
    left_copy(1 - y, c, 0, across, c).wait_recv()
    passed_on.start()
    pl.loop(early, pairs)(lambda q: relay(source(0), q))

    def take_left():
        left32[1 - y, c] = left[2 * c + 1 - y].astype(F32)
        theirs = left.at[pl.ds(2 * (1 - c), 2)]
        pltpu.make_async_remote_copy(
            src_ref=theirs, dst_ref=theirs, send_sem=lsend, recv_sem=lrecv.at[1],
            device_id={"row": row, "col": 1 - c}, device_id_type=MESH,
        ).wait_recv()
        for which in range(2):
            left32[which, 1 - c] = left[2 * (1 - c) + which].astype(F32)

    def ret_copy(part, there, slot):
        return pltpu.make_async_remote_copy(
            src_ref=part, dst_ref=there, send_sem=ret_send.at[slot], recv_sem=ret_recv.at[slot],
            device_id={"row": across, "col": c}, device_id_type=MESH,
        )

    def sums(which, blocks, pair, put):
        acc = [[None, None] for _ in range(rows)]
        for kc in range(2):
            wide = blocks[kc, pl.ds(pair * 2 * cols, 2 * cols), :].astype(F32)
            for kt in range(0, cols, 8):
                r = [wide[j * cols + kt : j * cols + kt + 8] for j in range(2)]
                for i in range(rows):
                    l = left32[which, kc, i * cols + kt : i * cols + kt + 8, :]
                    for j in range(2):
                        term = l * r[j]
                        acc[i][j] = term if acc[i][j] is None else acc[i][j] + term
        for i in range(rows):
            for j in range(2):
                put(i, j, jnp.sum(acc[i][j], axis=0, keepdims=True))

    def place(i, j, slot, pair, side, value):
        comb[i, pl.ds((slot * 2 + side) * rows + pair * 2 + j, 1), :] = value

    def order(t):
        inside = lax.rem(t + span - 1, span)
        return source(jnp.where((z >= low) & (z < low + span), inside, jnp.where(z > 0, t, span - 1 - t)))

    last = order(span - 1) - low

    lead = pairs // 2

    def combine(index):
        zs = order(index // pairs)
        pair = index % pairs
        slot = zs - low
        kept = jnp.where(far & (y == 1) & (slot == last), once, pairs)
        @pl.when((zs == z) & jnp.logical_not(passes(zs)))
        def _():
            block(right.at[slot, 1 - c, pl.ds(pair * step, step)], slot, pair, row).wait_recv()

        @pl.when((zs != z) & jnp.logical_not(passes(zs)))
        def _():
            block(both(slot, pair), slot, pair, row).wait_recv()

        def put_stage(i, j, value):
            stage[slot, pair, j * rows + i : j * rows + i + 1, :] = value

        @pl.when(pair < kept)
        def _():
            sums(1 - y, right.at[slot], pair, put_stage)
            ret_copy(stage.at[slot, pair], back.at[slot, pair], slot).start()

        sums(y, right.at[slot], pair, lambda i, j, value: place(i, j, slot, pair, y, value))

    rate = 2 if span == 2 else 1

    @pl.loop(0, -(-span * pairs // rate) + lead)
    def _(index):
        pl.when(index < (span - 1) * pairs)(lambda: relay(source(1 + index // pairs), index % pairs))
        pl.when(index == lead)(take_left)

        @pl.when(index >= lead)
        def _():
            pl.loop(rate * (index - lead), jnp.minimum(rate * (index - lead + 1), span * pairs))(combine)


    for way, cond, r, cc in ways:
        @pl.when(cond)
        def _(way=way, r=r, cc=cc):
            own_copy(way, r, cc, pl.ds(0, flat)).wait_send()
    sent = left.at[pl.ds(0, 3)]
    pltpu.make_async_remote_copy(
        src_ref=sent, dst_ref=sent, send_sem=lsend, recv_sem=lrecv.at[1],
        device_id={"row": row, "col": 1 - c}, device_id_type=MESH,
    ).wait_send()

    @pl.loop(0, span)
    def _(slot):
        @pl.when(passes(slot + low))
        def _():
            block(right.at[slot], slot, 0, row).wait_send()

    for count in (twice, LESS):
        @pl.when(helps & (once_there == pairs - count))
        def _(count=count):
            other_copy(shared - low, 0, count).wait_send()

    def collect(slot, part, stop):
        ret_copy(stage.at[slot, part], back.at[slot, part], slot).wait_recv()

        @pl.loop(0, stop)
        def _(pair):
            for i in range(rows):
                for j in range(2):
                    got = back[slot, pair, j * rows + i : j * rows + i + 1, :]
                    place(i, j, slot, pair, 1 - y, got)

    @pl.when(helped)
    def _():
        @pl.loop(0, pairs - once)
        def _(d):
            held = other.at[:, pl.ds(d * step, step)]
            pltpu.make_async_remote_copy(
                src_ref=held, dst_ref=held, send_sem=other_send, recv_sem=other_recv.at[d],
                device_id={"row": row, "col": c}, device_id_type=MESH,
            ).wait_recv()
            sums(y, other, d, lambda i, j, value: place(i, j, last, once + d, 1 - y, value))

    loads[4].wait()
    every = pl.ds(0, pairs)
    pl.loop(0, span - 1)(lambda t: collect(order(t) - low, every, pairs))
    pl.when(jnp.logical_not(helped))(lambda: collect(last, every, pairs))
    for count in (twice, LESS):
        some = pl.ds(0, pairs - count)
        pl.when(helped & (once == pairs - count))(lambda some=some, count=count: collect(last, some, pairs - count))
    @pl.when(row >= 0)
    def _():
        tri = layer_norm(comb[...].reshape(flat, hid)).astype(BF16)
        update = jnp.dot(tri, wo_ref[...], preferred_element_type=F32) * gate[...].reshape(flat, -1)
        out_ref[...] = update.astype(BF16).reshape(rows, cols, -1)

    @pl.loop(0, span)
    def _(slot):
        kept = far & (y == 1) & (slot == last)
        pl.when(jnp.logical_not(kept))(lambda: ret_copy(stage.at[slot], back.at[slot], slot).wait_send())
        for count in (twice, LESS):
            some = pl.ds(0, pairs - count)

            @pl.when(kept & (once == pairs - count))
            def _(some=some):
                ret_copy(stage.at[slot, some], back.at[slot, some], slot).wait_send()


def per_device(n, pair_rep, proj_weight, gate_weight, out_weight):
    rows, cols, channels = pair_rep.shape
    hid = out_weight.shape[0]
    flat = rows * cols
    pairs = rows // 2
    twice = TWICE
    span = n // 4
    padded = -(-2 * rows // 8) * 8
    vmem = pl.BlockSpec(memory_space=pltpu.VMEM)
    dma = pltpu.SemaphoreType.DMA
    return pl.pallas_call(
        functools.partial(kernel, n, rows, cols, pairs, twice),
        out_shape=pltpu.VMEM((rows, cols, channels), BF16),
        in_specs=[pl.BlockSpec(memory_space=pl.ANY)] * 4,
        out_specs=vmem,
        scratch_shapes=[
            pltpu.VMEM((flat, channels), BF16),
            pltpu.VMEM((2, channels, 2 * hid), BF16),
            pltpu.VMEM((channels, channels), BF16),
            pltpu.VMEM((hid, channels), BF16),
            pltpu.VMEM((flat, channels), BF16),
            dma((5,)),
            pltpu.VMEM((flat, hid), BF16),
            pltpu.VMEM((span, 2, flat, hid), BF16),
            pltpu.VMEM((4, flat, hid), BF16),
            pltpu.VMEM((2, 2, flat, hid), F32),
            pltpu.VMEM((rows, cols, hid), F32),
            pltpu.VMEM((rows, cols, channels), F32),
            pltpu.VMEM((span, pairs, padded, hid), F32),
            pltpu.VMEM((span, pairs, padded, hid), F32),
            pltpu.VMEM((2, twice * (flat // pairs), hid), BF16),
            dma((4,)),
            dma((span,)),
            dma((span, pairs)),
            dma,
            dma((2,)),
            dma((span,)),
            dma((span,)),
            dma,
            dma((twice,)),
        ],
        compiler_params=pltpu.CompilerParams(
            collective_id=0, has_side_effects=True, vmem_limit_bytes=60 * 1024 * 1024
        ),
    )(pair_rep.reshape(flat, channels), proj_weight, gate_weight, out_weight)


def solution(mesh):
    placed = (P(("groups", "row"), "col", None), P(), P(), P())
    return jax.shard_map(
        functools.partial(per_device, mesh.shape["row"]),
        mesh=mesh,
        in_specs=placed,
        out_specs=P(("groups", "row"), "col", None),
        check_vma=False,
    )
```

```python
import functools

import jax
import jax.numpy as jnp
from jax import lax
from jax.experimental import pallas as pl
from jax.experimental.pallas import tpu as pltpu
from jax.sharding import PartitionSpec as P

MESH = pl.DeviceIdType.MESH
F32 = jnp.float32
BF16 = jnp.bfloat16
TWICE = 3
LESS = 2


def layer_norm(values):
    average = jnp.mean(values, axis=-1, keepdims=True)
    centered = values - average
    spread = jnp.mean(centered * centered, axis=-1, keepdims=True)
    return centered * lax.rsqrt(spread + 1e-05)


def kernel(
    n, rows, cols, pairs, twice, x_hbm, wp_hbm, wg_hbm, wo_hbm, out_ref,
    x_ref, wp_ref, w_ref, normed, in_sem, own, right, left, left32, comb, gate, stage, back, other,
    own_send, fwd_send, recv, lsend, lrecv, ret_send, ret_recv, other_send, other_recv,
):
    hid, channels = wo_hbm.shape
    wg_ref, wo_ref = w_ref.at[pl.ds(0, channels)], w_ref.at[pl.ds(channels, hid)]
    flat = rows * cols
    step = flat // pairs
    loads = [pltpu.make_async_copy(x_hbm, x_ref, in_sem.at[0])]
    for k in (1, 0):
        cut = (slice(None), pl.ds(2 * hid * k, 2 * hid))
        loads.append(pltpu.make_async_copy(wp_hbm.at[cut], wp_ref.at[k], in_sem.at[len(loads)]))
    loads.append(pltpu.make_async_copy(wg_hbm, wg_ref, in_sem.at[3]))
    loads.append(pltpu.make_async_copy(wo_hbm, wo_ref, in_sem.at[3]))
    for load in loads:
        load.start()
    deep = n // 2
    span = deep // 2
    row, c = lax.axis_index("row"), lax.axis_index("col")
    z, y = row // 2, row % 2
    across = 2 * z + 1 - y
    has_up, has_down, has_far = z < deep - 1, z > 0, z > 2
    low = c * span
    dest = z // span
    my_slot = z - dest * span
    far = (z < low) | (z >= low + span)

    def first_twice(chip):
        return pairs - jnp.where((chip == 0) & (c == 1), twice, LESS)

    once = first_twice(z)
    helped = far & (y == 0)
    target = z + 1 - 2 * c
    helps = (y == 1) & jnp.where(c == 1, (z >= 1) & (z <= span), (z >= span - 1) & (z < deep - 1))
    barrier = pltpu.get_barrier_semaphore()

    def greet(r, cc):
        pl.semaphore_signal(barrier, inc=1, device_id={"row": r, "col": cc}, device_id_type=MESH)

    @pl.when((z + 3 < deep) & ((z + 3) // span == c))
    def _():
        for cc in range(2):
            greet(row + 6, cc)

    @pl.when(has_up)
    def _():
        for cc in range(2):
            greet(row + 2, cc)

    @pl.when(has_down)
    def _():
        for cc in range(2):
            greet(row - 2, cc)

    @pl.when(helped)
    def _():
        greet(2 * (z - 1 + 2 * c) + 1, c)

    greet(across, c)
    greet(row, 1 - c)

    def gated(values, k):
        proj = jnp.dot(values, wp_ref[k], preferred_element_type=F32)
        return (jax.nn.sigmoid(proj[:, :hid]) * proj[:, hid:]).astype(BF16)

    def prepare(p):
        here = pl.ds(p * step, step)
        values = layer_norm(x_ref[here, :].astype(F32)).astype(BF16)
        normed[here, :] = values
        own[here, :] = gated(values, 1)

    loads[0].wait()
    loads[1].wait()

    ways = ((0, has_far, row - 6, dest), (1, has_up, row + 2, dest), (2, has_down, row - 2, dest), (3, dest != c, row, dest))

    def own_copy(way, r, cc, part):
        return pltpu.make_async_remote_copy(
            src_ref=own.at[part], dst_ref=right.at[my_slot, c, part],
            send_sem=own_send.at[way], recv_sem=recv.at[my_slot, part.start // step],
            device_id={"row": r, "col": cc}, device_id_type=MESH,
        )

    for p in range(pairs):
        prepare(p)
    def compute_left():
        loads[2].wait()
        left[2 * c + y] = gated(normed[...], 0)

    @pl.when(has_up)
    def _():
        compute_left()
    pl.semaphore_wait(barrier, 2 + 2 * has_up.astype(jnp.int32) + 2 * has_down.astype(jnp.int32) + has_far.astype(jnp.int32) + helps.astype(jnp.int32))
    for p in range(pairs):
        for way, cond, r, cc in ways:
            @pl.when(cond)
            def _(way=way, r=r, cc=cc):
                own_copy(way, r, cc, pl.ds(p * step, step)).start()

    @pl.when(dest == c)
    def _():
        right[my_slot, c] = own[...]

    def left_copy(which, kc, arrive, r, cc):
        part = left.at[2 * kc + which]
        return pltpu.make_async_remote_copy(
            src_ref=part, dst_ref=part, send_sem=lsend, recv_sem=lrecv.at[arrive],
            device_id={"row": r, "col": cc}, device_id_type=MESH,
        )

    to_across = left_copy(y, c, 0, across, c)
    to_sibling = left_copy(y, c, 1, row, 1 - c)
    passed_on = left_copy(1 - y, c, 1, row, 1 - c)
    @pl.when(jnp.logical_not(has_up))
    def _():
        compute_left()
    to_across.start()
    to_sibling.start()
    left32[y, c] = left[2 * c + y].astype(F32)
    pltpu.make_async_copy(w_ref, w_ref, in_sem.at[3]).wait()
    opened = jax.nn.sigmoid(jnp.dot(normed[...], wg_ref[...], preferred_element_type=F32))
    gate[...] = opened.reshape(rows, cols, -1)

    def source(t):
        inside = low + lax.rem(z - low + t + 1 + deep, span)
        return jnp.where(z < low, low + t, jnp.where(z >= low + span, low + span - 1 - t, inside))

    def passes(zs):
        return ((zs < z) & has_up) | (((zs == z + 1) | (zs > z + 2)) & has_down)

    def block(part, slot, q, r):
        return pltpu.make_async_remote_copy(
            src_ref=part, dst_ref=part, send_sem=fwd_send.at[slot],
            recv_sem=recv.at[slot, q], device_id={"row": r, "col": c}, device_id_type=MESH,
        )

    def both(slot, q):
        return right.at[slot, :, pl.ds(q * step, step)]

    def other_copy(slot, d, count):
        return pltpu.make_async_remote_copy(
            src_ref=right.at[slot, :, pl.ds((once_there + d) * step, count * step)],
            dst_ref=other.at[:, pl.ds(d * step, count * step)],
            send_sem=other_send, recv_sem=other_recv.at[d], device_id={"row": 2 * target, "col": c}, device_id_type=MESH,
        )

    once_there = first_twice(target)
    shared = jnp.where(c == 1, jnp.where(target == 0, span, deep - 1), 0)

    def relay(zs, q):
        slot = zs - low
        to = jnp.where(zs < z, row + 2, row - 2)

        @pl.when(passes(zs))
        def _():
            doubled = helps & (zs == shared) & (q >= once_there)
            block(both(slot, q), slot, q, row).wait_recv()

            @pl.when(doubled)
            def _():
                other_copy(slot, q - once_there, 1).start()

            @pl.when(jnp.logical_not(doubled))
            def _():
                block(both(slot, q), slot, q, to).start()

            @pl.when(doubled & (q == pairs - 1))
            def _():
                pl.loop(once_there, pairs)(lambda p: block(both(slot, p), slot, p, to).start())

    early = jnp.where(c == 0, pairs, 0)
    pl.loop(0, early)(lambda q: relay(source(0), q))
    left_copy(1 - y, c, 0, across, c).wait_recv()
    passed_on.start()
    pl.loop(early, pairs)(lambda q: relay(source(0), q))

    def take_left():
        left32[1 - y, c] = left[2 * c + 1 - y].astype(F32)
        theirs = left.at[pl.ds(2 * (1 - c), 2)]
        pltpu.make_async_remote_copy(
            src_ref=theirs, dst_ref=theirs, send_sem=lsend, recv_sem=lrecv.at[1],
            device_id={"row": row, "col": 1 - c}, device_id_type=MESH,
        ).wait_recv()
        for which in range(2):
            left32[which, 1 - c] = left[2 * (1 - c) + which].astype(F32)

    def ret_copy(part, there, slot):
        return pltpu.make_async_remote_copy(
            src_ref=part, dst_ref=there, send_sem=ret_send.at[slot], recv_sem=ret_recv.at[slot],
            device_id={"row": across, "col": c}, device_id_type=MESH,
        )

    def sums(which, blocks, pair, put):
        acc = [[None, None] for _ in range(rows)]
        for kc in range(2):
            wide = blocks[kc, pl.ds(pair * 2 * cols, 2 * cols), :].astype(F32)
            for kt in range(0, cols, 8):
                r = [wide[j * cols + kt : j * cols + kt + 8] for j in range(2)]
                for i in range(rows):
                    l = left32[which, kc, i * cols + kt : i * cols + kt + 8, :]
                    for j in range(2):
                        term = l * r[j]
                        acc[i][j] = term if acc[i][j] is None else acc[i][j] + term
        for i in range(rows):
            for j in range(2):
                put(i, j, jnp.sum(acc[i][j], axis=0, keepdims=True))

    def place(i, j, slot, pair, side, value):
        comb[i, pl.ds((slot * 2 + side) * rows + pair * 2 + j, 1), :] = value

    def order(t):
        inside = lax.rem(t + span - 1, span)
        return source(jnp.where((z >= low) & (z < low + span), inside, jnp.where(z > 0, t, span - 1 - t)))

    last = order(span - 1) - low

    lead = 1

    def combine(index):
        zs = order(index // pairs)
        pair = index % pairs
        slot = zs - low
        kept = jnp.where(far & (y == 1) & (slot == last), once, pairs)
        @pl.when((zs == z) & jnp.logical_not(passes(zs)))
        def _():
            block(right.at[slot, 1 - c, pl.ds(pair * step, step)], slot, pair, row).wait_recv()

        @pl.when((zs != z) & jnp.logical_not(passes(zs)))
        def _():
            block(both(slot, pair), slot, pair, row).wait_recv()

        def put_stage(i, j, value):
            stage[slot, pair, j * rows + i : j * rows + i + 1, :] = value

        @pl.when(pair < kept)
        def _():
            sums(1 - y, right.at[slot], pair, put_stage)
            ret_copy(stage.at[slot, pair], back.at[slot, pair], slot).start()

        sums(y, right.at[slot], pair, lambda i, j, value: place(i, j, slot, pair, y, value))

    rate = 2 if span == 2 else 1

    @pl.loop(0, -(-span * pairs // rate) + lead)
    def _(index):
        pl.when(index < (span - 1) * pairs)(lambda: relay(source(1 + index // pairs), index % pairs))
        pl.when(index == lead)(take_left)

        @pl.when(index >= lead)
        def _():
            pl.loop(rate * (index - lead), jnp.minimum(rate * (index - lead + 1), span * pairs))(combine)


    for way, cond, r, cc in ways:
        @pl.when(cond)
        def _(way=way, r=r, cc=cc):
            own_copy(way, r, cc, pl.ds(0, flat)).wait_send()
    sent = left.at[pl.ds(0, 3)]
    pltpu.make_async_remote_copy(
        src_ref=sent, dst_ref=sent, send_sem=lsend, recv_sem=lrecv.at[1],
        device_id={"row": row, "col": 1 - c}, device_id_type=MESH,
    ).wait_send()

    @pl.loop(0, span)
    def _(slot):
        @pl.when(passes(slot + low))
        def _():
            block(right.at[slot], slot, 0, row).wait_send()

    for count in (twice, LESS):
        @pl.when(helps & (once_there == pairs - count))
        def _(count=count):
            other_copy(shared - low, 0, count).wait_send()

    def collect(slot, part, stop):
        ret_copy(stage.at[slot, part], back.at[slot, part], slot).wait_recv()

        @pl.loop(0, stop)
        def _(pair):
            for i in range(rows):
                for j in range(2):
                    got = back[slot, pair, j * rows + i : j * rows + i + 1, :]
                    place(i, j, slot, pair, 1 - y, got)

    @pl.when(helped)
    def _():
        @pl.loop(0, pairs - once)
        def _(d):
            held = other.at[:, pl.ds(d * step, step)]
            pltpu.make_async_remote_copy(
                src_ref=held, dst_ref=held, send_sem=other_send, recv_sem=other_recv.at[d],
                device_id={"row": row, "col": c}, device_id_type=MESH,
            ).wait_recv()
            sums(y, other, d, lambda i, j, value: place(i, j, last, once + d, 1 - y, value))

    every = pl.ds(0, pairs)
    pl.loop(0, span - 1)(lambda t: collect(order(t) - low, every, pairs))
    pl.when(jnp.logical_not(helped))(lambda: collect(last, every, pairs))
    for count in (twice, LESS):
        some = pl.ds(0, pairs - count)
        pl.when(helped & (once == pairs - count))(lambda some=some, count=count: collect(last, some, pairs - count))
    @pl.when(row >= 0)
    def _():
        tri = layer_norm(comb[...].reshape(flat, hid)).astype(BF16)
        update = jnp.dot(tri, wo_ref[...], preferred_element_type=F32) * gate[...].reshape(flat, -1)
        out_ref[...] = update.astype(BF16).reshape(rows, cols, -1)

    @pl.loop(0, span)
    def _(slot):
        kept = far & (y == 1) & (slot == last)
        pl.when(jnp.logical_not(kept))(lambda: ret_copy(stage.at[slot], back.at[slot], slot).wait_send())
        for count in (twice, LESS):
            some = pl.ds(0, pairs - count)

            @pl.when(kept & (once == pairs - count))
            def _(some=some):
                ret_copy(stage.at[slot, some], back.at[slot, some], slot).wait_send()


def per_device(n, pair_rep, proj_weight, gate_weight, out_weight):
    rows, cols, channels = pair_rep.shape
    hid = out_weight.shape[0]
    flat = rows * cols
    pairs = rows // 2
    twice = TWICE
    span = n // 4
    padded = -(-2 * rows // 8) * 8
    vmem = pl.BlockSpec(memory_space=pltpu.VMEM)
    dma = pltpu.SemaphoreType.DMA
    return pl.pallas_call(
        functools.partial(kernel, n, rows, cols, pairs, twice),
        out_shape=pltpu.VMEM((rows, cols, channels), BF16),
        in_specs=[pl.BlockSpec(memory_space=pl.ANY)] * 4,
        out_specs=vmem,
        scratch_shapes=[
            pltpu.VMEM((flat, channels), BF16),
            pltpu.VMEM((2, channels, 2 * hid), BF16),
            pltpu.VMEM((channels + hid, channels), BF16),
            pltpu.VMEM((flat, channels), BF16),
            dma((4,)),
            pltpu.VMEM((flat, hid), BF16),
            pltpu.VMEM((span, 2, flat, hid), BF16),
            pltpu.VMEM((4, flat, hid), BF16),
            pltpu.VMEM((2, 2, flat, hid), F32),
            pltpu.VMEM((rows, cols, hid), F32),
            pltpu.VMEM((rows, cols, channels), F32),
            pltpu.VMEM((span, pairs, padded, hid), F32),
            pltpu.VMEM((span, pairs, padded, hid), F32),
            pltpu.VMEM((2, twice * (flat // pairs), hid), BF16),
            dma((4,)),
            dma((span,)),
            dma((span, pairs)),
            dma,
            dma((2,)),
            dma((span,)),
            dma((span,)),
            dma,
            dma((twice,)),
        ],
        compiler_params=pltpu.CompilerParams(
            collective_id=0, has_side_effects=True, vmem_limit_bytes=60 * 1024 * 1024
        ),
    )(pair_rep.reshape(flat, channels), proj_weight, gate_weight, out_weight)


def solution(mesh):
    placed = (P(("groups", "row"), "col", None), P(), P(), P())
    return jax.shard_map(
        functools.partial(per_device, mesh.shape["row"]),
        mesh=mesh,
        in_specs=placed,
        out_specs=P(("groups", "row"), "col", None),
        check_vma=False,
    )
```

```python
import functools

import jax
import jax.numpy as jnp
from jax import lax
from jax.experimental import pallas as pl
from jax.experimental.pallas import tpu as pltpu
from jax.sharding import PartitionSpec as P

MESH = pl.DeviceIdType.MESH
F32 = jnp.float32
BF16 = jnp.bfloat16
TWICE = 3
LESS = 2


def layer_norm(values):
    average = jnp.mean(values, axis=-1, keepdims=True)
    centered = values - average
    spread = jnp.mean(centered * centered, axis=-1, keepdims=True)
    return centered * lax.rsqrt(spread + 1e-05)


def kernel(
    n, rows, cols, pairs, twice, x_hbm, wp_hbm, wg_hbm, wo_hbm, out_ref,
    x_ref, wp_ref, w_ref, normed, in_sem, own, right, left, left32, comb, gate, stage, back, other,
    own_send, fwd_send, recv, lsend, lrecv, ret_send, ret_recv, other_send, other_recv,
):
    hid, channels = wo_hbm.shape
    wg_ref, wo_ref = w_ref.at[pl.ds(0, channels)], w_ref.at[pl.ds(channels, hid)]
    flat = rows * cols
    step = flat // pairs
    loads = [pltpu.make_async_copy(x_hbm, x_ref, in_sem.at[0])]
    for k in (1, 0):
        cut = (slice(None), pl.ds(2 * hid * k, 2 * hid))
        loads.append(pltpu.make_async_copy(wp_hbm.at[cut], wp_ref.at[k], in_sem.at[len(loads)]))
    loads.append(pltpu.make_async_copy(wg_hbm, wg_ref, in_sem.at[3]))
    loads.append(pltpu.make_async_copy(wo_hbm, wo_ref, in_sem.at[3]))
    for load in loads:
        load.start()
    deep = n // 2
    span = deep // 2
    row, c = lax.axis_index("row"), lax.axis_index("col")
    z, y = row // 2, row % 2
    across = 2 * z + 1 - y
    has_up, has_down, has_far = z < deep - 1, z > 0, z > 2
    low = c * span
    dest = z // span
    my_slot = z - dest * span
    far = (z < low) | (z >= low + span)

    def first_twice(chip):
        return pairs - jnp.where((chip == 0) & (c == 1), twice, LESS)

    once = first_twice(z)
    helped = far & (y == 0)
    target = z + 1 - 2 * c
    helps = (y == 1) & jnp.where(c == 1, (z >= 1) & (z <= span), (z >= span - 1) & (z < deep - 1))
    barrier = pltpu.get_barrier_semaphore()

    def greet(r, cc):
        pl.semaphore_signal(barrier, inc=1, device_id={"row": r, "col": cc}, device_id_type=MESH)

    @pl.when((z + 3 < deep) & ((z + 3) // span == c))
    def _():
        for cc in range(2):
            greet(row + 6, cc)

    @pl.when(has_up)
    def _():
        for cc in range(2):
            greet(row + 2, cc)

    @pl.when(has_down)
    def _():
        for cc in range(2):
            greet(row - 2, cc)

    @pl.when(helped)
    def _():
        greet(2 * (z - 1 + 2 * c) + 1, c)

    greet(across, c)
    greet(row, 1 - c)

    def gated(values, k):
        proj = jnp.dot(values, wp_ref[k], preferred_element_type=F32)
        return (jax.nn.sigmoid(proj[:, :hid]) * proj[:, hid:]).astype(BF16)

    def prepare(p):
        here = pl.ds(p * step, step)
        values = layer_norm(x_ref[here, :].astype(F32)).astype(BF16)
        normed[here, :] = values
        own[here, :] = gated(values, 1)

    loads[0].wait()
    loads[1].wait()

    ways = ((0, has_far, row - 6, dest), (1, has_up, row + 2, dest), (2, has_down, row - 2, dest), (3, dest != c, row, dest))

    def own_copy(way, r, cc, part):
        return pltpu.make_async_remote_copy(
            src_ref=own.at[part], dst_ref=right.at[my_slot, c, part],
            send_sem=own_send.at[way], recv_sem=recv.at[my_slot, part.start // step],
            device_id={"row": r, "col": cc}, device_id_type=MESH,
        )

    for p in range(pairs):
        prepare(p)
    def compute_left():
        loads[2].wait()
        left[2 * c + y] = gated(normed[...], 0)

    @pl.when(has_up)
    def _():
        compute_left()
    pl.semaphore_wait(barrier, 2 + 2 * has_up.astype(jnp.int32) + 2 * has_down.astype(jnp.int32) + has_far.astype(jnp.int32) + helps.astype(jnp.int32))
    for p in range(pairs):
        for way, cond, r, cc in ways:
            @pl.when(cond)
            def _(way=way, r=r, cc=cc):
                own_copy(way, r, cc, pl.ds(p * step, step)).start()

    @pl.when(dest == c)
    def _():
        right[my_slot, c] = own[...]

    def left_copy(which, kc, arrive, r, cc):
        part = left.at[2 * kc + which]
        return pltpu.make_async_remote_copy(
            src_ref=part, dst_ref=part, send_sem=lsend, recv_sem=lrecv.at[arrive],
            device_id={"row": r, "col": cc}, device_id_type=MESH,
        )

    to_across = left_copy(y, c, 0, across, c)
    to_sibling = left_copy(y, c, 1, row, 1 - c)
    passed_on = left_copy(1 - y, c, 1, row, 1 - c)
    @pl.when(jnp.logical_not(has_up))
    def _():
        compute_left()
    to_across.start()
    to_sibling.start()
    left32[y, c] = left[2 * c + y].astype(F32)
    pltpu.make_async_copy(w_ref, w_ref, in_sem.at[3]).wait()
    opened = jax.nn.sigmoid(jnp.dot(normed[...], wg_ref[...], preferred_element_type=F32))
    gate[...] = opened.reshape(rows, cols, -1)

    def source(t):
        inside = low + lax.rem(z - low + t + 1 + deep, span)
        return jnp.where(z < low, low + t, jnp.where(z >= low + span, low + span - 1 - t, inside))

    def passes(zs):
        return ((zs < z) & has_up) | (((zs == z + 1) | (zs > z + 2)) & has_down)

    def block(part, slot, q, r):
        return pltpu.make_async_remote_copy(
            src_ref=part, dst_ref=part, send_sem=fwd_send,
            recv_sem=recv.at[slot, q], device_id={"row": r, "col": c}, device_id_type=MESH,
        )

    def both(slot, q):
        return right.at[slot, :, pl.ds(q * step, step)]

    def other_copy(slot, d, count):
        return pltpu.make_async_remote_copy(
            src_ref=right.at[slot, :, pl.ds((once_there + d) * step, count * step)],
            dst_ref=other.at[:, pl.ds(d * step, count * step)],
            send_sem=other_send, recv_sem=other_recv.at[d], device_id={"row": 2 * target, "col": c}, device_id_type=MESH,
        )

    once_there = first_twice(target)
    shared = jnp.where(c == 1, jnp.where(target == 0, span, deep - 1), 0)

    def relay(zs, q):
        slot = zs - low
        to = jnp.where(zs < z, row + 2, row - 2)

        @pl.when(passes(zs))
        def _():
            doubled = helps & (zs == shared) & (q >= once_there)
            block(both(slot, q), slot, q, row).wait_recv()

            @pl.when(doubled)
            def _():
                other_copy(slot, q - once_there, 1).start()

            @pl.when(jnp.logical_not(doubled))
            def _():
                block(both(slot, q), slot, q, to).start()

            @pl.when(doubled & (q == pairs - 1))
            def _():
                pl.loop(once_there, pairs)(lambda p: block(both(slot, p), slot, p, to).start())

    early = jnp.where(c == 0, pairs, 0)
    pl.loop(0, early)(lambda q: relay(source(0), q))
    left_copy(1 - y, c, 0, across, c).wait_recv()
    passed_on.start()
    pl.loop(early, pairs)(lambda q: relay(source(0), q))

    def take_left():
        left32[1 - y, c] = left[2 * c + 1 - y].astype(F32)
        theirs = left.at[pl.ds(2 * (1 - c), 2)]
        pltpu.make_async_remote_copy(
            src_ref=theirs, dst_ref=theirs, send_sem=lsend, recv_sem=lrecv.at[1],
            device_id={"row": row, "col": 1 - c}, device_id_type=MESH,
        ).wait_recv()
        for which in range(2):
            left32[which, 1 - c] = left[2 * (1 - c) + which].astype(F32)

    def ret_copy(part, there, slot):
        return pltpu.make_async_remote_copy(
            src_ref=part, dst_ref=there, send_sem=ret_send.at[slot], recv_sem=ret_recv.at[slot],
            device_id={"row": across, "col": c}, device_id_type=MESH,
        )

    def sums(which, blocks, pair, put):
        acc = [[None, None] for _ in range(rows)]
        for kc in range(2):
            wide = blocks[kc, pl.ds(pair * 2 * cols, 2 * cols), :].astype(F32)
            for kt in range(0, cols, 8):
                r = [wide[j * cols + kt : j * cols + kt + 8] for j in range(2)]
                for i in range(rows):
                    l = left32[which, kc, i * cols + kt : i * cols + kt + 8, :]
                    for j in range(2):
                        term = l * r[j]
                        acc[i][j] = term if acc[i][j] is None else acc[i][j] + term
        for i in range(rows):
            for j in range(2):
                put(i, j, jnp.sum(acc[i][j], axis=0, keepdims=True))

    def place(i, j, slot, pair, side, value):
        comb[i, pl.ds((slot * 2 + side) * rows + pair * 2 + j, 1), :] = value

    def order(t):
        inside = lax.rem(t + span - 1, span)
        return source(jnp.where((z >= low) & (z < low + span), inside, jnp.where(z > 0, t, span - 1 - t)))

    last = order(span - 1) - low

    lead = 1

    def combine(index):
        zs = order(index // pairs)
        pair = index % pairs
        slot = zs - low
        kept = jnp.where(far & (y == 1) & (slot == last), once, pairs)
        @pl.when((zs == z) & jnp.logical_not(passes(zs)))
        def _():
            block(right.at[slot, 1 - c, pl.ds(pair * step, step)], slot, pair, row).wait_recv()

        @pl.when((zs != z) & jnp.logical_not(passes(zs)))
        def _():
            block(both(slot, pair), slot, pair, row).wait_recv()

        def put_stage(i, j, value):
            stage[slot, pair, j * rows + i : j * rows + i + 1, :] = value

        @pl.when(pair < kept)
        def _():
            sums(1 - y, right.at[slot], pair, put_stage)
            ret_copy(stage.at[slot, pair], back.at[slot, pair], slot).start()

        sums(y, right.at[slot], pair, lambda i, j, value: place(i, j, slot, pair, y, value))

    rate = 2 if span == 2 else 1

    @pl.loop(0, -(-span * pairs // rate) + lead)
    def _(index):
        pl.when(index < (span - 1) * pairs)(lambda: relay(source(1 + index // pairs), index % pairs))
        pl.when(index == lead)(take_left)

        @pl.when(index >= lead)
        def _():
            pl.loop(rate * (index - lead), jnp.minimum(rate * (index - lead + 1), span * pairs))(combine)


    for way, cond, r, cc in ways:
        @pl.when(cond)
        def _(way=way, r=r, cc=cc):
            own_copy(way, r, cc, pl.ds(0, flat)).wait_send()
    sent = left.at[pl.ds(0, 3)]
    pltpu.make_async_remote_copy(
        src_ref=sent, dst_ref=sent, send_sem=lsend, recv_sem=lrecv.at[1],
        device_id={"row": row, "col": 1 - c}, device_id_type=MESH,
    ).wait_send()

    passing = sum(passes(s + low).astype(jnp.int32) for s in range(span))
    for count in range(1, span + 1):
        @pl.when(passing == count)
        def _(count=count):
            block(right.at[pl.ds(0, count)], 0, 0, row).wait_send()

    for count in (twice, LESS):
        @pl.when(helps & (once_there == pairs - count))
        def _(count=count):
            other_copy(shared - low, 0, count).wait_send()

    def collect(slot, part, stop):
        ret_copy(stage.at[slot, part], back.at[slot, part], slot).wait_recv()

        @pl.loop(0, stop)
        def _(pair):
            for i in range(rows):
                for j in range(2):
                    got = back[slot, pair, j * rows + i : j * rows + i + 1, :]
                    place(i, j, slot, pair, 1 - y, got)

    @pl.when(helped)
    def _():
        @pl.loop(0, pairs - once)
        def _(d):
            held = other.at[:, pl.ds(d * step, step)]
            pltpu.make_async_remote_copy(
                src_ref=held, dst_ref=held, send_sem=other_send, recv_sem=other_recv.at[d],
                device_id={"row": row, "col": c}, device_id_type=MESH,
            ).wait_recv()
            sums(y, other, d, lambda i, j, value: place(i, j, last, once + d, 1 - y, value))

    every = pl.ds(0, pairs)
    pl.loop(0, span - 1)(lambda t: collect(order(t) - low, every, pairs))
    pl.when(jnp.logical_not(helped))(lambda: collect(last, every, pairs))
    for count in (twice, LESS):
        some = pl.ds(0, pairs - count)
        pl.when(helped & (once == pairs - count))(lambda some=some, count=count: collect(last, some, pairs - count))
    @pl.when(row >= 0)
    def _():
        tri = layer_norm(comb[...].reshape(flat, hid)).astype(BF16)
        update = jnp.dot(tri, wo_ref[...], preferred_element_type=F32) * gate[...].reshape(flat, -1)
        out_ref[...] = update.astype(BF16).reshape(rows, cols, -1)

    @pl.loop(0, span)
    def _(slot):
        kept = far & (y == 1) & (slot == last)
        pl.when(jnp.logical_not(kept))(lambda: ret_copy(stage.at[slot], back.at[slot], slot).wait_send())
        for count in (twice, LESS):
            some = pl.ds(0, pairs - count)

            @pl.when(kept & (once == pairs - count))
            def _(some=some):
                ret_copy(stage.at[slot, some], back.at[slot, some], slot).wait_send()


def per_device(n, pair_rep, proj_weight, gate_weight, out_weight):
    rows, cols, channels = pair_rep.shape
    hid = out_weight.shape[0]
    flat = rows * cols
    pairs = rows // 2
    twice = TWICE
    span = n // 4
    padded = -(-2 * rows // 8) * 8
    vmem = pl.BlockSpec(memory_space=pltpu.VMEM)
    dma = pltpu.SemaphoreType.DMA
    return pl.pallas_call(
        functools.partial(kernel, n, rows, cols, pairs, twice),
        out_shape=pltpu.VMEM((rows, cols, channels), BF16),
        in_specs=[pl.BlockSpec(memory_space=pl.ANY)] * 4,
        out_specs=vmem,
        scratch_shapes=[
            pltpu.VMEM((flat, channels), BF16),
            pltpu.VMEM((2, channels, 2 * hid), BF16),
            pltpu.VMEM((channels + hid, channels), BF16),
            pltpu.VMEM((flat, channels), BF16),
            dma((4,)),
            pltpu.VMEM((flat, hid), BF16),
            pltpu.VMEM((span, 2, flat, hid), BF16),
            pltpu.VMEM((4, flat, hid), BF16),
            pltpu.VMEM((2, 2, flat, hid), F32),
            pltpu.VMEM((rows, cols, hid), F32),
            pltpu.VMEM((rows, cols, channels), F32),
            pltpu.VMEM((span, pairs, padded, hid), F32),
            pltpu.VMEM((span, pairs, padded, hid), F32),
            pltpu.VMEM((2, twice * (flat // pairs), hid), BF16),
            dma((4,)),
            dma,
            dma((span, pairs)),
            dma,
            dma((2,)),
            dma((span,)),
            dma((span,)),
            dma,
            dma((twice,)),
        ],
        compiler_params=pltpu.CompilerParams(
            collective_id=0, has_side_effects=True, vmem_limit_bytes=60 * 1024 * 1024
        ),
    )(pair_rep.reshape(flat, channels), proj_weight, gate_weight, out_weight)


def solution(mesh):
    placed = (P(("groups", "row"), "col", None), P(), P(), P())
    return jax.shard_map(
        functools.partial(per_device, mesh.shape["row"]),
        mesh=mesh,
        in_specs=placed,
        out_specs=P(("groups", "row"), "col", None),
        check_vma=False,
    )
```
